32 devices in a mesh: row: 8 (over y, x, core), col: 4 (over z).
Axes of the slice: x: 2, y: 2, z: 4, core: 2. Of those that a mesh axis runs over, the one named last changes fastest.
Arguments:
- image: bfloat16 [512, 512, 512], P('row', 'col'), may hold values from -6 to 6
- w_local: bfloat16 [3, 3, 512, 128], replicated, may hold values from -0.09375 to 0.09375
- w_cross: bfloat16 [3, 3, 128, 384], replicated, may hold values from -0.1875 to 0.1875
- w_spec: bfloat16 [768, 768], replicated, may hold values from -0.21875 to 0.21875
Outputs:
- result: bfloat16 [512, 512, 512], P('row', 'col')
The draws below stay inside these ranges and needn't reach their ends.
All inputs are finite; a program needn't handle non-finite values.
Results may differ from the reference program's by a relative error of at most 0.0055.
Values may be sent and summed in bfloat16 or wider, within the bound.
A program may use at most 192 MiB of HBM per device.

```python
import jax
import jax.numpy as jnp
from jax import lax

H = 512
W = 512
CL = 128
CG = 384
C = 512
CS = 768


def block_levels(rng, dims, pieces, low, high):
    level = 1.0
    for dim, parts in pieces:
        steps = jax.random.uniform(jax.random.fold_in(jax.random.fold_in(rng, 6), dim), (parts,), jnp.float32, low / len(pieces), high / len(pieces))
        level = level * jnp.repeat(jnp.exp(steps), dims[dim] // parts).reshape((-1,) + (1,) * (len(dims) - 1 - dim))
    return level


def scatter_about(stream_key, shape, scale, bound, pieces=(), kind=jnp.bfloat16):
    values = jax.random.normal(stream_key, shape, jnp.float32) * scale
    if len(pieces) > 0:
        values = block_levels(stream_key, shape, pieces, -0.22, 0.18) * values
    return jnp.clip(values, min=-bound, max=bound).astype(kind)


def setup_inputs(seed: int = 0) -> dict:
    splits = jax.random.split(jax.random.key(seed), 5)
    return {
        "image": scatter_about(splits[0], (H, W, C), 1.0, 6.0, ((0, 8), (1, 4))),
        "w_local": scatter_about(splits[1], (3, 3, C, CL), (9 * C) ** -0.5, 0.09375),
        "w_cross": scatter_about(splits[2], (3, 3, CL, CG), (9 * CL) ** -0.5, 0.1875),
        "w_spec": scatter_about(splits[3], (CS, CS), CS ** -0.5, 0.21875),
    }


def conv_three(features, weight):
    height, width = features.shape[0], features.shape[1]
    padded = jnp.pad(features, ((1, 1), (1, 1), (0, 0)))
    total = jnp.zeros((height, width, weight.shape[3]), jnp.float32)
    for shift_y in range(3):
        for shift_x in range(3):
            window = padded[shift_y:shift_y + height, shift_x:shift_x + width]
            part = jnp.dot(window.reshape(height * width, -1), weight[shift_y, shift_x], preferred_element_type=jnp.float32)
            total = total + part.reshape(height, width, -1)
    return total


def round_half(values):
    return lax.optimization_barrier(values.astype(jnp.bfloat16)).astype(jnp.float32)


def reference(image, w_local, w_cross, w_spec):
    local_out = conv_three(image, w_local)
    cross_out = conv_three(image[..., :CL], w_cross)
    glob = image[..., CL:].astype(jnp.float32)
    rowspec = jnp.fft.rfft(glob, axis=1, norm="ortho")
    row_field = round_half(rowspec.real) + 1j * round_half(rowspec.imag)
    spectrum = jnp.fft.fft(row_field, axis=0, norm="ortho")
    bins = W // 2 + 1
    stacked = jnp.concatenate([spectrum.real, spectrum.imag], axis=-1).astype(jnp.bfloat16)
    mixed = jnp.dot(stacked.reshape(H * bins, CS), w_spec, preferred_element_type=jnp.float32)
    mixed = jnp.maximum(mixed, 0.0).reshape(H, bins, CS)
    centred = mixed - jnp.sum(mixed, axis=(0, 1)) / (H * bins)
    field = centred[..., :CG] + 1j * centred[..., CG:]
    colinv = jnp.fft.ifft(field, axis=0, norm="ortho")
    col_field = round_half(colinv.real) + 1j * round_half(colinv.imag)
    back = jnp.fft.irfft(col_field, n=W, axis=1, norm="ortho")
    result = jnp.concatenate([local_out, cross_out + back.astype(jnp.float32)], axis=-1)
    return result.astype(jnp.bfloat16)
```

```python
import jax
import jax.numpy as jnp
import numpy as np
from jax import lax
from jax.sharding import PartitionSpec as P

BOTH = ("row", "col")


def rounded(table):
    return np.asarray(table, np.float32).astype(jnp.bfloat16)


def column_table(height):
    freq = np.arange(height // 2)
    angle = 2.0 * np.pi * (np.outer(freq, np.arange(height)) % height) / height
    table = np.stack([np.cos(angle), -np.sin(angle)], axis=1)
    table[0, 1] = 1.0 - 2.0 * (np.arange(height) % 2)
    return rounded(table.reshape(height, height) / np.sqrt(height))


def width_order(nrow, ncol, width):
    part = width // (nrow * ncol)
    r, c, i = np.meshgrid(np.arange(nrow), np.arange(ncol), np.arange(part), indexing="ij")
    return (c * (width // ncol) + r * part + i).reshape(-1)


def width_tables(order, width, padded):
    half = width // 2
    count = width + 2
    plain = np.concatenate([np.arange(width), [0, half]])
    packed = np.concatenate([np.arange(half + 1), np.arange(half + 1)])
    rows = np.arange(count)
    out = []
    for freq in (plain, packed):
        angle = 2.0 * np.pi * (np.outer(freq, order) % width) / width
        pair = np.zeros((2, padded, width))
        pair[0, :count] = np.cos(angle) / np.sqrt(width)
        pair[1, :count] = np.sin(angle) / np.sqrt(width)
        out.append(rounded(pair))
    sign = np.where(rows <= half, 1.0, -1.0)
    scale_plain = np.where(np.isin(rows, [0, half, width, width + 1]), 1.0, 2.0)
    scale_packed = np.where(np.isin(packed, [0, half]), 1.0, 2.0)
    extra = padded - count
    pad = lambda v: np.pad(v, (0, extra))
    upper = pad((rows <= half).astype(np.float64))
    lower = pad((rows > half).astype(np.float64))
    return out[0], out[1], pad(sign), upper, lower, pad(scale_plain), pad(scale_packed)


def assembled(pair, blocks, xp):
    cosine, sine = pair[0], pair[1]
    pick = {"c": cosine, "s": sine}
    lines = []
    for line in blocks:
        lines.append(xp.concatenate([pick[k] * v[:, None] for k, v in line], axis=1))
    return xp.concatenate(lines, axis=0)


def extended(cells, sides, width):
    for axis, dim in sides:
        count = lax.axis_size(axis)
        ends = count - 1
        head = lax.slice_in_dim(cells, 0, width, axis=dim)
        tail = lax.slice_in_dim(cells, cells.shape[dim] - width, cells.shape[dim], axis=dim)
        cells = jnp.concatenate(
            [
                lax.ppermute(tail, axis, [(i, (i + 1) % count) for i in range(ends)]),
                cells,
                lax.ppermute(head, axis, [((i + 1) % count, i) for i in range(ends)]),
            ],
            axis=dim,
        )
    return cells


def conv(padded, weight):
    return lax.conv_general_dilated(
        padded[None],
        weight,
        (1, 1),
        "VALID",
        dimension_numbers=("NHWC", "HWIO", "NHWC"),
        preferred_element_type=jnp.float32,
    )[0]


def product(form, left, right):
    return jnp.einsum(form, left, right, preferred_element_type=jnp.float32)


def global_branch(glob, w_spec):
    nrow, ncol = lax.axis_size("row"), lax.axis_size("col")
    count = nrow * ncol
    height, width, ch = glob.shape[0] * nrow, glob.shape[1] * ncol, glob.shape[2]
    bins = height // (2 * count)
    padded = -(-(width + 2) // 16) * 16

    columns = lax.all_to_all(glob, "row", split_axis=1, concat_axis=0, tiled=True)

    col_np = column_table(height)
    plain_np, packed_np, sign, upper, lower, scale_plain, scale_packed = width_tables(
        width_order(nrow, ncol, width), width, padded
    )
    ones = np.ones_like(sign)
    plain_form = ((("c", ones), ("s", ones)), (("s", -sign), ("c", sign)))
    packed_form = ((("c", upper), ("c", lower)), (("s", -upper), ("s", -lower)))

    def row_sums(pair, form, scale):
        table = assembled(pair.astype(np.float64), form, np) * np.tile(scale, 2)[:, None]
        return np.stack([table[:padded].sum(0), table[padded:].sum(0)], axis=1).astype(np.float32)

    def cast_form(form):
        return [[(k, jnp.asarray(rounded(v))) for k, v in line] for line in form]

    col_table = jnp.asarray(col_np)
    is_first = lax.axis_index(BOTH) == 0
    special = (is_first & (jnp.arange(bins) == 0))[:, None, None]
    table = jnp.where(
        special,
        assembled(jnp.asarray(packed_np), cast_form(packed_form), jnp)[None],
        assembled(jnp.asarray(plain_np), cast_form(plain_form), jnp)[None],
    )
    scale = jnp.where(
        special,
        jnp.asarray(scale_packed, jnp.float32)[None, :, None],
        jnp.asarray(scale_plain, jnp.float32)[None, :, None],
    )
    sums = jnp.where(
        special,
        jnp.asarray(row_sums(packed_np, packed_form, scale_packed))[None],
        jnp.asarray(row_sums(plain_np, plain_form, scale_plain))[None],
    )

    field = product("uh,hwc->uwc", col_table, columns).astype(jnp.bfloat16)
    lines = lax.all_to_all(field, BOTH, split_axis=0, concat_axis=1, tiled=True)
    lines = lines.reshape(bins, 2 * width, ch)
    spectrum = product("bmk,bkc->bmc", table, lines).astype(jnp.bfloat16)
    stacked = jnp.concatenate([spectrum[:, :padded], spectrum[:, padded:]], axis=-1)
    mixed = jnp.maximum(product("bvc,co->bvo", stacked, w_spec), 0.0)
    own_sum = jnp.sum(mixed, axis=(0, 1))
    every = lax.all_to_all(
        jnp.broadcast_to(own_sum[None], (count, 2 * ch)), BOTH, split_axis=0, concat_axis=0, tiled=True
    )
    mean = jnp.sum(every, axis=0) / (height * (width // 2 + 1))
    scaled = (mixed * scale).astype(jnp.bfloat16)
    scaled = jnp.concatenate([scaled[..., :ch], scaled[..., ch:]], axis=1)
    offset = sums[:, :, :1] * mean[:ch] + sums[:, :, 1:] * mean[ch:]
    inverted = (product("bkm,bkc->bmc", table, scaled) - offset).astype(jnp.bfloat16)
    inverted = inverted.reshape(2 * bins, width, ch)
    back = lax.all_to_all(inverted, BOTH, split_axis=1, concat_axis=0, tiled=True)
    rows = product("uh,uwc->hwc", col_table, back).astype(jnp.bfloat16)
    return lax.all_to_all(rows, "row", split_axis=0, concat_axis=1, tiled=True)


def body(image, w_local, w_cross, w_spec):
    local_chan = w_cross.shape[2]
    spectral = global_branch(image[..., local_chan:], w_spec)
    padded = extended(image, (("row", 0), ("col", 1)), 1)
    local_out = conv(padded, w_local)
    cross_out = conv(padded[..., :local_chan], w_cross)
    result = jnp.concatenate(
        [local_out.astype(jnp.bfloat16), (cross_out + spectral).astype(jnp.bfloat16)], axis=-1
    )
    return result


def solution(mesh):
    in_specs = (P("row", "col", None), P(), P(), P())
    out_specs = P("row", "col", None)
    return jax.shard_map(body, mesh=mesh, in_specs=in_specs, out_specs=out_specs, check_vma=False)
```
